512 devices in a mesh: gx: 8 (over y_lo, core), gy: 8 (over z), gz: 8 (over x, y_hi).
Axes of the slice: x: 4, y: 8 (y_hi: 2, y_lo: 4; y = y_hi * 4 + y_lo), z: 8, core: 2. Of those that a mesh axis runs over, the one named last changes fastest.
Arguments:
- particles: float32 [26, 262144], P(None, ('gx', 'gy', 'gz')), may hold values from -4 to 4, as said below
- block_ids: int32 [262144], P(('gx', 'gy', 'gz')), may hold values from 0 to 7
- node_offsets: int32 [262144], P(('gx', 'gy', 'gz')), may hold values from 0 to 511
- live_count: int32 [512], P(('gx', 'gy', 'gz')), may hold values from 64 to 512, as said below
- migrations: int32 [6, 4096], P(None, ('gx', 'gy', 'gz')), may hold values from 0 to 511, as said below
Outputs:
- moved_records: float32 [26, 262144], P(None, ('gx', 'gy', 'gz'))
The draws below stay inside these ranges and needn't reach their ends.
Inputs may be any that keep to these rules, and one draw needn't show every extreme that they name: `live_count`: slots below a domain's count are live; some domain is full and some holds exactly 64. `migrations`: the 48 entries of one domain are distinct slots, each live in that domain. `particles`: entries of F lie within 0.15 of the identity's; positions within a cell between -0.5 and 0.5; masses between 0.5 and 2; plastic ratios between 0.9 and 1.1.
All inputs are finite; a program needn't handle non-finite values.
Results may differ from the reference program's by a relative error of at most 0.0003.
Values sent between devices are 32-bit elements; how exact they have to be, the bound alone decides.
No kernel may reach another device: no remote copies, remote signals or barrier semaphores. Data moves between devices by JAX's collectives and lax.ppermute only.
A program may use at most 64 MiB of HBM per device.

```python
import math
import jax
import jax.numpy as jnp
import numpy as np
from jax import lax

BLK = 2
P_DEV = 512
CAP = 8
PARTICLES = 262144
N_GX = 8
N_GY = 8
N_GZ = 8
DEVICES = 512


def migration_plan(key):
    key_count, key_jitter, key_full, key_score = jax.random.split(jax.random.fold_in(key, 11), 4)
    levels = jax.random.randint(key_count, (DEVICES,), 0, 4)
    jitter = jax.random.randint(key_jitter, (DEVICES,), 0, P_DEV // 16 + 1)
    counts = jnp.minimum(P_DEV // jnp.left_shift(jnp.int32(1), levels) + jitter, P_DEV)
    fullest = jax.random.randint(key_full, (), 0, DEVICES)
    device_index = jnp.arange(DEVICES, dtype=jnp.int32)
    counts = jnp.where(device_index == fullest, P_DEV, counts)
    counts = jnp.where(device_index == (fullest + 1) % DEVICES, P_DEV // 8, counts).astype(jnp.int32)
    slot_index = jnp.arange(P_DEV, dtype=jnp.int32)
    scores = jax.random.randint(key_score, (DEVICES, P_DEV), 0, 1 << 14) * P_DEV + slot_index[None, :] + 1
    scores = jnp.where(slot_index[None, :] < counts[:, None], scores, scores + (1 << 30))
    forced = (device_index[:, None] == fullest) & ((slot_index[None, :] == 0) | (slot_index[None, :] == P_DEV - 1))
    scores = jnp.where(forced, 0, scores)
    ranking = jnp.argsort(scores, axis=1, stable=True)[:, :6 * CAP].astype(jnp.int32)
    plan_table = ranking.reshape(DEVICES, 6, CAP).transpose(1, 0, 2).reshape(6, DEVICES * CAP)
    return (counts, plan_table)


def draw_live_count(key, part):
    return migration_plan(key)[0]


def draw_migrations(key, part):
    return migration_plan(key)[1]


def draw_particles(key, part):
    subkeys = jax.random.split(jax.random.fold_in(key, 5), 6)
    velocity = jnp.clip(jax.random.normal(subkeys[0], (3, PARTICLES)), -4.0, 4.0)
    affine = jnp.clip(0.6 * jax.random.normal(subkeys[1], (9, PARTICLES)), -3.0, 3.0)
    deform = jnp.eye(3, dtype=jnp.float32).reshape(9, 1) + jax.random.uniform(subkeys[2], (9, PARTICLES), minval=-0.15, maxval=0.15)
    fraction = jax.random.uniform(subkeys[3], (3, PARTICLES), minval=-0.5, maxval=0.5)
    particle_mass = jnp.exp(jax.random.uniform(subkeys[4], (1, PARTICLES), minval=math.log(0.5), maxval=math.log(2.0)))
    plastic = jax.random.uniform(subkeys[5], (1, PARTICLES), minval=0.9, maxval=1.1)
    return jnp.concatenate([velocity, affine, deform, fraction, particle_mass, plastic]).astype(jnp.float32)


def plant(drawn, rng, smallest, top_value):
    index_at = [jax.random.randint(jax.random.fold_in(rng, axis), (), 0, length) for axis, length in enumerate(drawn.shape)]
    longest = drawn.shape.index(max(drawn.shape))
    next_to = index_at[:longest] + [(index_at[longest] + 1) % drawn.shape[longest]] + index_at[longest + 1:]
    return drawn.at[tuple(index_at)].set(smallest).at[tuple(next_to)].set(top_value)


def cumulative_ranks(number_of, skew):
    weights = [(1 << 20) // math.isqrt(rank ** skew) + 1 for rank in range(1, number_of + 1)]
    spread = 1 + sum(weights) // (1 << 30)
    return np.cumsum(np.array([max(1, weight // spread) for weight in weights]))


def ranked_ids(rng, extent, count, lean):
    table = cumulative_ranks(count, lean)
    lot = jax.random.randint(jax.random.fold_in(rng, 1), extent, 0, int(table[count - 1]))
    standing = jnp.searchsorted(jnp.asarray(table, jnp.int32), lot, side="right")
    return jax.random.permutation(jax.random.fold_in(rng, 2), count)[standing].astype(jnp.int32)


def setup_inputs(seed: int = 0) -> dict:
    key_list = jax.random.split(jax.random.key(seed), 6)
    particles = draw_particles(jax.random.fold_in(key_list[5], 71), 0)
    block_ids = plant(ranked_ids(key_list[1], (PARTICLES,), BLK ** 3, 2), jax.random.fold_in(key_list[1], 3), 0, (BLK ** 3) - 1).astype(jnp.int32)
    node_offsets = plant(jax.random.randint(key_list[2], (PARTICLES,), 0, 512), jax.random.fold_in(key_list[2], 1), 0, 511).astype(jnp.int32)
    live_count = draw_live_count(jax.random.fold_in(key_list[5], 71), 0)
    migrations = draw_migrations(jax.random.fold_in(key_list[5], 71), 0)
    return dict(particles=particles, block_ids=block_ids, node_offsets=node_offsets, live_count=live_count, migrations=migrations)


time_step = 0.05
stress_gain = 0.2
shear_zero = 5.0
bulk_zero = 5.0
harden_rate = 10.0
mass_floor = 0.1
gravity = 9.8


def matrix_product(left_side, right_side):
    rows_out = []
    for row_id in range(3):
        entries = []
        for col_id in range(3):
            entries.append(left_side[row_id, 0] * right_side[0, col_id] + left_side[row_id, 1] * right_side[1, col_id] + left_side[row_id, 2] * right_side[2, col_id])
        rows_out.append(jnp.stack(entries))
    return jnp.stack(rows_out)


def matrix_vector(matrix, vector):
    return jnp.stack([matrix[row_id, 0] * vector[0] + matrix[row_id, 1] * vector[1] + matrix[row_id, 2] * vector[2] for row_id in range(3)])


def matrix_transpose(matrix):
    return jnp.transpose(matrix, (1, 0, 2))


def determinant(matrix):
    return (matrix[0, 0] * (matrix[1, 1] * matrix[2, 2] - matrix[1, 2] * matrix[2, 1])
            - matrix[0, 1] * (matrix[1, 0] * matrix[2, 2] - matrix[1, 2] * matrix[2, 0])
            + matrix[0, 2] * (matrix[1, 0] * matrix[2, 1] - matrix[1, 1] * matrix[2, 0]))


def kirchhoff(deform, plastic):
    identity = jnp.eye(3, dtype=deform.dtype)[:, :, None]
    rotation = deform
    for iteration in range(5):
        rotation = 0.5 * matrix_product(rotation, 3.0 * identity - matrix_product(matrix_transpose(rotation), rotation))
    volume = determinant(deform)
    harden = jnp.exp(harden_rate * (1.0 - plastic))
    shear_mod = shear_zero * harden
    bulk_mod = bulk_zero * harden
    return 2.0 * shear_mod * matrix_product(deform - rotation, matrix_transpose(deform)) + (bulk_mod * (volume - 1.0) * volume) * identity


def spline_weights(fraction):
    return jnp.stack([0.5 * (0.5 - fraction) ** 2, 0.75 - fraction * fraction, 0.5 * (0.5 + fraction) ** 2])


def anchor_nodes(block_ids, node_offsets, blocks):
    corner = jnp.stack([block_ids // (blocks * blocks), (block_ids // blocks) % blocks, block_ids % blocks])
    inside = jnp.stack([node_offsets // 64, (node_offsets // 8) % 8, node_offsets % 8])
    return 8 * corner + inside + 8


def stencil_point(fraction, anchor, weights_axis, padded, stencil_id):
    delta_node = (stencil_id // 9 - 1, (stencil_id // 3) % 3 - 1, stencil_id % 3 - 1)
    weight = weights_axis[delta_node[0] + 1, 0] * weights_axis[delta_node[1] + 1, 1] * weights_axis[delta_node[2] + 1, 2]
    displace = jnp.stack([delta_node[axis_id] - fraction[axis_id] for axis_id in range(3)])
    node_pos = [anchor[axis_id] + delta_node[axis_id] for axis_id in range(3)]
    block_flat = ((node_pos[0] // 8) * padded + node_pos[1] // 8) * padded + node_pos[2] // 8
    flat_index = block_flat * 512 + (node_pos[0] % 8) * 64 + (node_pos[1] % 8) * 8 + node_pos[2] % 8
    return flat_index, weight, displace


def scatter_grid(particles, block_ids, node_offsets, living, blocks):
    padded = blocks + 2
    fraction = particles[21:24]
    affine = particles[3:12].reshape(3, 3, -1)
    deform = particles[12:21].reshape(3, 3, -1)
    particle_mass = particles[24] * living
    coupling = (particles[24] * affine - stress_gain * kirchhoff(deform, particles[25])) * living
    momentum = particle_mass * particles[0:3]
    anchor = anchor_nodes(block_ids, node_offsets, blocks)
    weights_axis = spline_weights(fraction)
    grid_sums = jnp.zeros((4, padded * padded * padded * 512), particles.dtype)
    for stencil_id in range(27):
        flat_index, weight, displace = stencil_point(fraction, anchor, weights_axis, padded, stencil_id)
        pushed = weight * (momentum + matrix_vector(coupling, displace))
        values = jnp.concatenate([(weight * particle_mass)[None], pushed])
        grid_sums = grid_sums.at[:, flat_index].add(values)
    return grid_sums.reshape(4, padded, padded, padded, 512)


def grid_update(totals):
    velocity = totals[1:4] / jnp.maximum(totals[0:1], mass_floor)
    return velocity.at[2].add(-time_step * gravity)


def gather_grid(particles, block_ids, node_offsets, living, blocks, velocity_grid):
    padded = blocks + 2
    fraction = particles[21:24]
    deform = particles[12:21].reshape(3, 3, -1)
    anchor = anchor_nodes(block_ids, node_offsets, blocks)
    weights_axis = spline_weights(fraction)
    flattened = velocity_grid.reshape(3, -1)
    new_velocity = jnp.zeros_like(fraction)
    new_affine = jnp.zeros_like(deform)
    for stencil_id in range(27):
        flat_index, weight, displace = stencil_point(fraction, anchor, weights_axis, padded, stencil_id)
        sampled = weight * flattened[:, flat_index]
        new_velocity = new_velocity + sampled
        new_affine = new_affine + 4.0 * sampled[:, None, :] * displace[None, :, :]
    new_deform = deform + time_step * matrix_product(new_affine, deform)
    new_fraction = fraction + time_step * new_velocity
    record_rows = jnp.concatenate([new_velocity, new_affine.reshape(9, -1), new_deform.reshape(9, -1), new_fraction, particles[24:26]])
    return record_rows * living


def fold_axis(grid_sums, domain_axis, block_axis, blocks):
    lower_side = lax.slice_in_dim(grid_sums, 0, 1, axis=block_axis)
    upper_side = lax.slice_in_dim(grid_sums, blocks + 1, blocks + 2, axis=block_axis)
    centre = lax.slice_in_dim(grid_sums, 1, blocks + 1, axis=block_axis)
    first_block = lax.slice_in_dim(centre, 0, 1, axis=block_axis) + jnp.roll(upper_side, 1, axis=domain_axis)
    last_block = lax.slice_in_dim(centre, blocks - 1, blocks, axis=block_axis) + jnp.roll(lower_side, -1, axis=domain_axis)
    middle = lax.slice_in_dim(centre, 1, blocks - 1, axis=block_axis)
    return jnp.concatenate([first_block, middle, last_block], axis=block_axis)


def pad_axis(velocity_field, domain_axis, block_axis, blocks):
    lower_pad = jnp.roll(lax.slice_in_dim(velocity_field, blocks - 1, blocks, axis=block_axis), 1, axis=domain_axis)
    upper_pad = jnp.roll(lax.slice_in_dim(velocity_field, 0, 1, axis=block_axis), -1, axis=domain_axis)
    return jnp.concatenate([lower_pad, velocity_field, upper_pad], axis=block_axis)


def reference(particles, block_ids, node_offsets, live_count, migrations):
    domains = N_GX * N_GY * N_GZ
    padded = BLK + 2
    per_record = particles.reshape(26, domains, P_DEV).transpose(1, 0, 2)
    per_block = block_ids.reshape(domains, P_DEV)
    per_offset = node_offsets.reshape(domains, P_DEV)
    slot_index = jnp.arange(P_DEV, dtype=jnp.int32)
    living = (slot_index[None, :] < live_count[:, None]).astype(particles.dtype)
    grids = jax.vmap(lambda record_rows, chosen, placed, alive_rows: scatter_grid(record_rows, chosen, placed, alive_rows, BLK))(per_record, per_block, per_offset, living)
    grids = grids.reshape(N_GX, N_GY, N_GZ, 4, padded, padded, padded, 512)
    totals = fold_axis(fold_axis(fold_axis(grids, 0, 4, BLK), 1, 5, BLK), 2, 6, BLK)
    owned_velocity = jax.vmap(grid_update)(totals.reshape(domains, 4, BLK, BLK, BLK, 512))
    owned_velocity = owned_velocity.reshape(N_GX, N_GY, N_GZ, 3, BLK, BLK, BLK, 512)
    padded_velocity = pad_axis(pad_axis(pad_axis(owned_velocity, 0, 4, BLK), 1, 5, BLK), 2, 6, BLK)
    padded_velocity = padded_velocity.reshape(domains, 3, padded, padded, padded, 512)
    updated = jax.vmap(lambda record_rows, chosen, placed, alive_rows, velocity_grid: gather_grid(record_rows, chosen, placed, alive_rows, BLK, velocity_grid))(per_record, per_block, per_offset, living, padded_velocity)
    plan_table = migrations.reshape(6, domains, CAP).transpose(1, 0, 2).reshape(domains, 6 * CAP)
    outgoing = jax.vmap(lambda record_rows, chosen: record_rows[:, chosen])(updated, plan_table)
    outgoing = outgoing.reshape(N_GX, N_GY, N_GZ, 26, 6, CAP)
    arrivals = []
    for direction_id in range(6):
        direction = 1 if direction_id % 2 == 0 else -1
        arrivals.append(jnp.roll(outgoing[:, :, :, :, direction_id, :], direction, axis=direction_id // 2))
    arrived = jnp.stack(arrivals, axis=4).reshape(domains, 26, 6 * CAP)
    moved = jax.vmap(lambda record_rows, chosen, incoming: record_rows.at[:, chosen].set(incoming))(updated, plan_table, arrived)
    return moved.transpose(1, 0, 2).reshape(26, domains * P_DEV)
```

```python
import jax
import jax.numpy as jnp
from jax import lax
from jax.experimental import pallas as pl
from jax.experimental.pallas import tpu as pltpu
from jax.sharding import PartitionSpec as P

SLOTS = 512
NODES = 18
PITCH = 24
ROWS = 4 * NODES
LANES = PITCH * NODES
PAIR = 2 * PITCH
FACES = 6
CAP = 8

time_step = 0.05
stress_gain = 0.2
shear_zero = 5.0
bulk_zero = 5.0
harden_rate = 10.0
mass_floor = 0.1
gravity = 9.8
f32 = jnp.float32
bf16 = jnp.bfloat16
INTERPRET = False


def product(a, b):
    return [[a[i][0] * b[0][j] + a[i][1] * b[1][j] + a[i][2] * b[2][j] for j in range(3)] for i in range(3)]


def transpose(a):
    return [[a[j][i] for j in range(3)] for i in range(3)]


def kirchhoff(deform, plastic):
    rotation = deform
    for _ in range(5):
        square = product(transpose(rotation), rotation)
        rest = [[(3.0 if i == j else 0.0) - square[i][j] for j in range(3)] for i in range(3)]
        rotation = product([[0.5 * e for e in row] for row in rotation], rest)
    d = deform
    volume = (
        d[0][0] * (d[1][1] * d[2][2] - d[1][2] * d[2][1])
        - d[0][1] * (d[1][0] * d[2][2] - d[1][2] * d[2][0])
        + d[0][2] * (d[1][0] * d[2][1] - d[1][1] * d[2][0])
    )
    harden = jnp.exp(harden_rate * (1.0 - plastic))
    shear = 2.0 * shear_zero * harden
    bulk = bulk_zero * harden * (volume - 1.0) * volume
    strain = [[d[i][j] - rotation[i][j] for j in range(3)] for i in range(3)]
    tau = product(strain, transpose(d))
    return [[shear * tau[i][j] + (bulk if i == j else 0.0) for j in range(3)] for i in range(3)]


def split2(x):
    hi = x.astype(bf16)
    return hi, (x - hi.astype(f32)).astype(bf16)


def split3(x):
    hi = x.astype(bf16)
    rest = x - hi.astype(f32)
    mid = rest.astype(bf16)
    return hi, mid, (rest - mid.astype(f32)).astype(bf16)


def spline(f):
    return (0.5 * (0.5 - f) * (0.5 - f), 0.75 - f * f, 0.5 * (0.5 + f) * (0.5 + f))


def anchors(bid, off):
    return (
        8 * (bid >> 2) + (off >> 6) + 1,
        8 * ((bid >> 1) & 1) + ((off >> 3) & 7) + 1,
        8 * (bid & 1) + (off & 7) + 1,
    )


def tables(index, anchor, w):
    d = index - anchor
    low = jnp.where(d == -1, w[0], 0.0)
    high = jnp.where(d == 1, w[2], 0.0)
    return low + high + jnp.where(d == 0, w[1], 0.0), high - low


def wide(x, rows):
    return jnp.broadcast_to(x, (rows, x.shape[1]))


def z_tables(anchor, f):
    w = [wide(e, 8) for e in spline(f)]
    a = wide(anchor, 8)
    sub = lax.broadcasted_iota(jnp.int32, (8, SLOTS), 0) >> 2
    return [tables(2 * t + sub, a, w) for t in range(ROWS // 8)]


def dot_nt(a, b):
    return lax.dot_general(a, b, (((1,), (1,)), ((), ())), preferred_element_type=f32)


def dot_nn(a, b):
    return lax.dot_general(a, b, (((1,), (0,)), ((), ())), preferred_element_type=f32)


def scatter_kernel(live, part, bid, off, low, high, grid, bhi, blo, ahi, alo):
    row = lambda r: part[r : r + 1, :]
    slot = lax.broadcasted_iota(jnp.int32, (1, SLOTS), 1)
    living = (slot < live[0]).astype(f32)
    v = [row(i) for i in range(3)]
    affine = [[row(3 + 3 * i + j) for j in range(3)] for i in range(3)]
    deform = [[row(12 + 3 * i + j) for j in range(3)] for i in range(3)]
    f = [row(21 + i) for i in range(3)]
    mass = row(24)
    tau = kirchhoff(deform, row(25))
    coupling = [[(mass * affine[i][j] - stress_gain * tau[i][j]) * living for j in range(3)] for i in range(3)]
    mass = mass * living
    base = [
        mass * v[i] - (coupling[i][0] * f[0] + coupling[i][1] * f[1] + coupling[i][2] * f[2])
        for i in range(3)
    ]
    none = jnp.zeros_like(mass)
    base8 = jnp.concatenate([mass] + base + [mass] + base)
    along = [jnp.concatenate(([none] + [coupling[i][j] for i in range(3)]) * 2) for j in range(3)]
    ax, ay, az = anchors(bid[...], off[...])

    firsts, seconds, thirds = [], [], []
    for weight, shift in z_tables(az, f[2]):
        firsts.append(base8 * weight + along[2] * shift)
        seconds.append(along[0] * weight)
        thirds.append(along[1] * weight)
    pad = jnp.zeros((8, SLOTS), f32)
    for kind, parts in enumerate((firsts, seconds, thirds)):
        hi, lo = split2(jnp.concatenate(parts + [pad]))
        ahi[:, kind * SLOTS : (kind + 1) * SLOTS] = hi
        alo[:, kind * SLOTS : (kind + 1) * SLOTS] = lo

    wx = [wide(e, 8) for e in spline(f[0])]
    axw = wide(ax, 8)
    wy, sy = tables(
        lax.broadcasted_iota(jnp.int32, (PITCH, SLOTS), 0),
        wide(ay, PITCH),
        [wide(e, PITCH) for e in spline(f[1])],
    )
    for pair in range(NODES // 2):
        kinds = ([], [], [])
        for ix in (2 * pair, 2 * pair + 1):
            w, s = tables(ix, axw, wx)
            w, s = (jnp.concatenate([e] * (PITCH // 8)) for e in (w, s))
            kinds[0].append(w * wy)
            kinds[1].append(s * wy)
            kinds[2].append(w * sy)
        for kind, parts in enumerate(kinds):
            hi, lo = split2(jnp.concatenate(parts))
            bhi[pair * PAIR : (pair + 1) * PAIR, kind * SLOTS : (kind + 1) * SLOTS] = hi
            blo[pair * PAIR : (pair + 1) * PAIR, kind * SLOTS : (kind + 1) * SLOTS] = lo

    total = dot_nt(ahi[...], bhi[...]) + dot_nt(alo[...], bhi[...]) + dot_nt(ahi[...], blo[...])
    grid[...] = total[:ROWS]
    low[...] = total[:8]
    high[...] = total[ROWS - 8 : ROWS]


def z_kernel(grid, from_low, from_high, out, low, high):
    out[...] = grid[...]
    out[0:8, :] = grid[0:8, :] + from_low[...]
    out[ROWS - 8 : ROWS, :] = grid[ROWS - 8 : ROWS, :] + from_high[...]
    low[...] = out[:, 0:PAIR]
    high[...] = out[:, LANES - PAIR : LANES]


def picks(first):
    lane = lax.broadcasted_iota(jnp.int32, (LANES, 128), 0)
    col = lax.broadcasted_iota(jnp.int32, (LANES, 128), 1)
    return (lane == PITCH * (col >> 1) + first + (col & 1)).astype(f32).astype(bf16)


def x_kernel(grid, from_low, from_high, out, low, high):
    out[...] = grid[...]
    out[:, 0:PAIR] = grid[:, 0:PAIR] + from_low[...]
    out[:, LANES - PAIR : LANES] = grid[:, LANES - PAIR : LANES] + from_high[...]
    parts = split3(out[...])
    for first, slab in ((0, low), (NODES - 2, high)):
        chosen = picks(first)
        slab[...] = sum(dot_nn(part, chosen) for part in parts)


def gather_kernel(
    live, grid, from_low, from_high, bhi, blo, part, bid, off, moving,
    out, o0, o1, o2, o3, o4, o5,
):
    total = grid[...]
    for first, slab in ((0, from_low), (NODES - 2, from_high)):
        chosen = picks(first)
        for piece in split3(slab[...]):
            total = total + dot_nt(piece, chosen)
    channel = lax.broadcasted_iota(jnp.int32, (ROWS, LANES), 0) & 3
    mass = jnp.where(channel == 0, total, 0.0)
    mass = mass + pltpu.roll(mass, 1, 0)
    mass = mass + pltpu.roll(mass, 2, 0)
    velocity = total / jnp.maximum(mass, mass_floor)
    velocity = jnp.where(channel == 3, velocity - time_step * gravity, velocity)
    vhi, vlo = split2(velocity)
    right = bhi[...]
    read = dot_nn(vhi, right) + dot_nn(vlo, right) + dot_nn(vhi, blo[...])

    row = lambda r: part[r : r + 1, :]
    f = [row(21 + i) for i in range(3)]
    az = anchors(bid[...], off[...])[2]
    sums = [None] * 4
    for t, (weight, shift) in enumerate(z_tables(az, f[2])):
        rows = slice(8 * t, 8 * t + 8)
        first = read[rows, 0:SLOTS]
        terms = (
            first * weight,
            read[rows, SLOTS : 2 * SLOTS] * weight,
            read[rows, 2 * SLOTS : 3 * SLOTS] * weight,
            first * shift,
        )
        sums = [b if a is None else a + b for a, b in zip(sums, terms)]
    sums = [e[0:4] + e[4:8] for e in sums]
    slot = lax.broadcasted_iota(jnp.int32, (1, SLOTS), 1)
    living = (slot < live[0]).astype(f32)
    v = [sums[0][i + 1 : i + 2] for i in range(3)]
    affine = [[4.0 * (sums[1 + j][i + 1 : i + 2] - v[i] * f[j]) for j in range(3)] for i in range(3)]
    deform = [[row(12 + 3 * i + j) for j in range(3)] for i in range(3)]
    change = product(affine, deform)
    rows = v + [e for r in affine for e in r]
    rows += [deform[i][j] + time_step * change[i][j] for i in range(3) for j in range(3)]
    rows += [f[i] + time_step * v[i] for i in range(3)]
    rows += [row(24), row(25)]
    record = jnp.concatenate([e * living for e in rows] + [jnp.zeros((6, SLOTS), f32)])
    out[...] = record[0:26]

    lane = lax.broadcasted_iota(jnp.int32, (FACES * CAP, SLOTS), 1)
    selector = (lane == moving[...]).astype(f32).astype(bf16)
    leaving = sum(dot_nt(selector, piece) for piece in split3(record))
    for face, o in enumerate((o0, o1, o2, o3, o4, o5)):
        o[...] = leaving[face * CAP : (face + 1) * CAP]


def place_kernel(record, moving, a0, a1, a2, a3, a4, a5, out):
    arrived = jnp.concatenate([a[...] for a in (a0, a1, a2, a3, a4, a5)])
    lane = lax.broadcasted_iota(jnp.int32, (FACES * CAP, SLOTS), 1)
    selector = (lane == moving[...]).astype(f32)
    taken = jnp.sum(selector, axis=0, keepdims=True)
    selector = selector.astype(bf16)
    placed = sum(
        lax.dot_general(piece, selector, (((0,), (0,)), ((), ())), preferred_element_type=f32)
        for piece in split3(arrived)
    )
    out[...] = jnp.where(taken > 0.5, placed[0:26], record[...])


def call(kernel, name, outs, ins, scratch=(), scalar=False):
    vmem = pl.BlockSpec(memory_space=pltpu.VMEM)
    specs = [vmem] * len(ins)
    if scalar:
        specs[0] = pl.BlockSpec(memory_space=pltpu.SMEM)
    return pl.pallas_call(
        kernel,
        name=name,
        out_shape=[jax.ShapeDtypeStruct(s, d) for s, d in outs],
        in_specs=specs,
        out_specs=[vmem] * len(outs),
        scratch_shapes=list(scratch),
        interpret=INTERPRET,
    )(*ins)


def swap(low, high, axis):
    n = lax.axis_size(axis)
    forward = [(i, (i + 1) % n) for i in range(n)]
    backward = [(t, s) for s, t in forward]
    return lax.ppermute(high, axis, forward), lax.ppermute(low, axis, backward)


def body(particles, block_ids, node_offsets, live_count, migrations):
    bid = block_ids.reshape(1, SLOTS)
    off = node_offsets.reshape(1, SLOTS)
    moving = migrations.reshape(FACES * CAP, 1)
    row8 = ((8, LANES), f32)
    whole = ((ROWS, LANES), f32)
    table = ((LANES, 3 * SLOTS), bf16)
    low, high, grid, bhi, blo = call(
        scatter_kernel, "scatter", [row8, row8, whole, table, table],
        [live_count, particles, bid, off],
        [pltpu.VMEM((ROWS + 8, 3 * SLOTS), bf16)] * 2, scalar=True,
    )
    before, after = swap(low, high, "gz")
    side = ((ROWS, PAIR), f32)
    grid, low, high = call(z_kernel, "zfold", [whole, side, side], [grid, before, after])
    before, after = swap(low, high, "gx")
    edge = ((ROWS, 128), f32)
    grid, low, high = call(x_kernel, "xfold", [whole, edge, edge], [grid, before, after])
    before, after = swap(low, high, "gy")
    record, *leaving = call(
        gather_kernel, "gather", [((26, SLOTS), f32)] + [((CAP, 32), f32)] * FACES,
        [live_count, grid, before, after, bhi, blo, particles, bid, off, moving], scalar=True,
    )
    arrived = []
    for face, axis in ((0, "gx"), (2, "gy"), (4, "gz")):
        arrived += swap(leaving[face + 1], leaving[face], axis)
    (out,) = call(place_kernel, "place", [((26, SLOTS), f32)], [record, moving] + arrived)
    return out


def solution(mesh):
    return jax.shard_map(
        body,
        mesh=mesh,
        in_specs=(
            P(None, ("gx", "gy", "gz")),
            P(("gx", "gy", "gz")),
            P(("gx", "gy", "gz")),
            P(("gx", "gy", "gz")),
            P(None, ("gx", "gy", "gz")),
        ),
        out_specs=P(None, ("gx", "gy", "gz")),
        check_vma=False,
    )
```
